512 devices in a mesh: pair: 32 (over x, y), ph: 16 (over z, core).
Axes of the slice: x: 4, y: 8, z: 8, core: 2. Of those that a mesh axis runs over, the one named last changes fastest.
Arguments:
- t_cycle: float32 [8, 512, 8192], P(None, 'pair', 'ph'), may hold values from -6 to 6
- w_cycle: float32 [8, 8192, 4096], P(None, 'ph', 'pair'), may hold values from -0.1875 to 0.1875
- occ_energy: float32 [64], replicated, may hold values from -1.5 to -0.5
- vir_energy: float32 [8, 128], replicated, may hold values from 0.2 to 1.5
- occ_irrep: int32 [64], replicated, may hold values from 0 to 7
- vir_count: int32 [8], replicated, may hold values from 1 to 128, 640 in all
Outputs:
- increment: float32 [8, 512, 4096], P(None, 'ph', 'pair')
The draws below stay inside these ranges and needn't reach their ends.
Inputs may be any that keep to these rules, and one draw needn't show every extreme that they name: `occ_irrep`: irrep labels combine by exclusive or. `vir_count`: the counts sum to 640; one irrep fills all 128 slots.
All inputs are finite; a program needn't handle non-finite values.
Results may differ from the reference program's by a relative error of at most 0.000075.
Values sent between devices are 32-bit elements; how exact they have to be, the bound alone decides.
No kernel may reach another device: no remote copies, remote signals or barrier semaphores. Data moves between devices by JAX's collectives and lax.ppermute only.
A program may use at most 64 MiB of HBM per device.

```python
import math
import jax
import jax.numpy as jnp
import numpy as np
from jax import lax

IRREPS = 8
OCCUPIED = 64
VIRT_CAP = 128
VIRTUALS = 640
ROW_OCC = 4
COL_OCC = 32
ROWS = 512
PAIRS = 8192
COLS = 4096


def set_ends(result, own_key, low, top_value):
    spot = [jax.random.randint(jax.random.fold_in(own_key, axis), (), 0, length) for axis, length in enumerate(result.shape)]
    widest = result.shape.index(max(result.shape))
    neighbour = spot[:widest] + [(spot[widest] + 1) % result.shape[widest]] + spot[widest + 1:]
    return result.at[tuple(spot)].set(low).at[tuple(neighbour)].set(top_value)


def steps_of(rng, dims, cuts, smallest, high):
    factor_of = 1.0
    for dim, parts in cuts:
        draws = jax.random.uniform(jax.random.fold_in(jax.random.fold_in(rng, 6), dim), (parts,), jnp.float32, smallest / len(cuts), high / len(cuts))
        factor_of = factor_of * jnp.repeat(jnp.exp(draws), dims[dim] // parts).reshape((-1,) + (1,) * (len(dims) - 1 - dim))
    return factor_of


def profile(amount, total, bound, skew):
    portions = [(1 << 20) // math.isqrt(grade ** skew) + 1 for grade in range(2, amount + 1)]
    rest, given = total - bound - (amount - 1), [1] * (amount - 1)
    while rest > 0:
        movable = [i for i in range(amount - 1) if given[i] < bound]
        mass, left = sum([portions[i] for i in movable]), rest
        for i in movable:
            more = min(bound - given[i], max(1, left * portions[i] // mass), rest)
            given[i] = given[i] + more
            rest = rest - more
    return np.array([bound] + given)


def ragged_sizes(rng, amount, total, bound, lean):
    if amount == 2:
        one = jax.random.randint(rng, (), max(1, total - bound), min(bound, total - 1) + 1)
        return jnp.stack([one, total - one])
    sizes = jnp.asarray(profile(amount, total, bound, lean), jnp.int32)
    pairs = (amount - 1) // 2
    giver, receiver = sizes[1:1 + 2 * pairs:2], sizes[2:2 + 2 * pairs:2]
    margin = jnp.minimum(giver - 1, bound - receiver)
    passed = jax.random.randint(jax.random.fold_in(rng, 1), (pairs,), 0, 1 << 20) % (margin + 1)
    sizes = sizes.at[1:1 + 2 * pairs:2].set(giver - passed).at[2:2 + 2 * pairs:2].set(receiver + passed)
    return sizes[jax.random.permutation(jax.random.fold_in(rng, 2), amount)]


def bell_draw(own_key, shape, width, most, shards=(), kind=jnp.bfloat16):
    array = jax.random.normal(own_key, shape, jnp.float32) * width
    if len(shards) > 0:
        array = steps_of(own_key, shape, shards, -0.22, 0.18) * array
    return jnp.clip(array, min=-most, max=most).astype(kind)


def setup_inputs(seed: int = 0) -> dict:
    splits = jax.random.split(jax.random.key(seed), 7)
    t_cycle = bell_draw(splits[0], (IRREPS, ROWS, PAIRS), 1.0, 6.0, ((1, 32), (2, 16)), jnp.float32)
    w_cycle = bell_draw(splits[1], (IRREPS, PAIRS, COLS), (PAIRS // IRREPS) ** -0.5, 0.1875, ((1, 16), (2, 32)), jnp.float32)
    occ_energy = jnp.clip(jax.random.uniform(splits[2], (OCCUPIED,), jnp.float32, -1.5, -0.5), -1.5, -0.5)
    vir_energy = jnp.clip(jax.random.uniform(splits[3], (IRREPS, VIRT_CAP), jnp.float32, 0.2, 1.5), 0.2, 1.5)
    occ_irrep = set_ends(jax.random.randint(splits[4], (OCCUPIED,), 0, IRREPS), jax.random.fold_in(splits[4], 1), 0, IRREPS - 1).astype(jnp.int32)
    vir_count = ragged_sizes(splits[5], IRREPS, VIRTUALS, VIRT_CAP, 1).astype(jnp.int32)
    return dict(t_cycle=t_cycle, w_cycle=w_cycle, occ_energy=occ_energy, vir_energy=vir_energy, occ_irrep=occ_irrep, vir_count=vir_count)


def reference(t_cycle, w_cycle, occ_energy, vir_energy, occ_irrep, vir_count):
    slot_ids = jnp.arange(VIRT_CAP, dtype=jnp.int32)
    irreps = jnp.arange(IRREPS, dtype=jnp.int32)
    symmetry = jnp.bitwise_xor(occ_irrep[None, :], irreps[:, None]).astype(jnp.int32)
    counts = vir_count[symmetry]
    live_slot = (slot_ids[None, None, :] < counts[:, :, None]).astype(jnp.float32)
    vir_ener = vir_energy[symmetry]
    mask_pair = live_slot.reshape(IRREPS, PAIRS)
    mask_row = live_slot[:, :ROW_OCC].reshape(IRREPS, ROWS)
    mask_col = live_slot[:, :COL_OCC].reshape(IRREPS, COLS)
    e_row = (occ_energy[None, :ROW_OCC, None] - vir_ener[:, :ROW_OCC]).reshape(IRREPS, ROWS)
    e_col = (occ_energy[None, :COL_OCC, None] - vir_ener[:, :COL_OCC]).reshape(IRREPS, COLS)

    def contract(irrep):
        masked = w_cycle[irrep] * mask_pair[irrep][:, None]
        return jnp.dot(t_cycle[irrep], masked, precision=lax.Precision.HIGHEST, preferred_element_type=jnp.float32)

    cycle = lax.map(contract, irreps)
    return mask_row[:, :, None] * mask_col[:, None, :] * cycle / (e_row[:, :, None] + e_col[:, None, :])
```

```python
import jax
import jax.numpy as jnp
import numpy as np
from jax import lax
from jax.experimental import pallas as pl
from jax.experimental.pallas import tpu as pltpu
from jax.sharding import Mesh, PartitionSpec as P

IRREPS = 8
SLOTS = 128
NX, NY, NZ, NC = 4, 8, 8, 2
AXES = ("x", "y", "z", "c")
K_LOCAL = 512
OFFSETS = (0, 1, 7, 4, 2, 5, 6, 3)


def shift_y(value, step):
    ids = np.arange(NX * NY * NZ * NC).reshape(NX, NY, NZ, NC)
    targets = np.roll(ids, -step, axis=1)
    return lax.ppermute(value, AXES, list(zip(ids.ravel().tolist(), targets.ravel().tolist())))


def split(value):
    high = value.astype(jnp.bfloat16)
    low = (value - high.astype(jnp.float32)).astype(jnp.bfloat16)
    return high, low


def product_body(occ_ref, count_ref, t0, t1, t2, t3, t45, t67, w_ref, out_ref, t_high, t_low, w_high, w_low):
    y = lax.axis_index("y")
    z = lax.axis_index("z")
    g = lax.axis_index("x") * NC + lax.axis_index("c")

    @pl.when(pl.program_id(0) == 0)
    def _():
        blocks = [(t0, 0), (t1, 0), (t2, 0), (t3, 0), (t45, 0), (t45, 8), (t67, 0), (t67, 8)]
        for slot, (ref, first) in enumerate(blocks):
            for i in range(NX):
                for c in range(NC):
                    high, low = split(ref[first + i * NC + c])
                    rows = pl.ds((slot * NX + i) * 16, 16)
                    cols = pl.ds(c * K_LOCAL, K_LOCAL)
                    t_high[rows, cols] = high
                    t_low[rows, cols] = low

    slots = lax.broadcasted_iota(jnp.int32, (SLOTS, SLOTS), 0)
    for c in range(NC):
        for k in range(4):
            live = slots < count_ref[jnp.bitwise_xor(occ_ref[z * 8 + c * 4 + k], g)]
            for half in range(2):
                part = jnp.where(live, w_ref[half * NC + c, pl.ds(k * SLOTS, SLOTS), :], 0.0)
                high, low = split(part)
                rows = pl.ds(c * K_LOCAL + k * SLOTS, SLOTS)
                cols = pl.ds(half * SLOTS, SLOTS)
                w_high[rows, cols] = high
                w_low[rows, cols] = low

    def dot(a, b):
        return jnp.dot(a[...], b[...], preferred_element_type=jnp.float32)

    total = dot(t_high, w_low) + dot(t_low, w_high) + dot(t_high, w_high)
    for slot, offset in enumerate(OFFSETS):
        first = pl.multiple_of(lax.rem(y + offset, NY) * 16, 16)
        for i in range(NX):
            for half in range(2):
                rows = slice((slot * NX + i) * 16, (slot * NX + i + 1) * 16)
                out_ref[half, i, pl.ds(first, 16), :] = total[rows, half * SLOTS : (half + 1) * SLOTS]


def product(occ_irrep, vir_count, blocks, w):
    whole = lambda shape: pl.BlockSpec(shape, lambda n: (0,) * len(shape))
    return pl.pallas_call(
        product_body,
        grid=(2,),
        in_specs=[
            pl.BlockSpec(memory_space=pltpu.SMEM),
            pl.BlockSpec(memory_space=pltpu.SMEM),
            *[whole(b.shape) for b in blocks],
            pl.BlockSpec((4, K_LOCAL, SLOTS), lambda n: (n, 0, 0)),
        ],
        out_specs=pl.BlockSpec((2, NX, SLOTS, SLOTS), lambda n: (n, 0, 0, 0)),
        out_shape=jax.ShapeDtypeStruct((NX, NX, SLOTS, SLOTS), jnp.float32),
        scratch_shapes=[
            pltpu.VMEM((512, 2 * K_LOCAL), jnp.bfloat16),
            pltpu.VMEM((512, 2 * K_LOCAL), jnp.bfloat16),
            pltpu.VMEM((2 * K_LOCAL, 2 * SLOTS), jnp.bfloat16),
            pltpu.VMEM((2 * K_LOCAL, 2 * SLOTS), jnp.bfloat16),
        ],
        name="product",
    )(occ_irrep, vir_count, *blocks, w)


def finish_body(parts_ref, factor_ref, out_ref):
    for x in range(NX):
        for c in range(NC):
            total = parts_ref[x, 0, c]
            for z in range(1, NZ):
                total = total + parts_ref[x, z, c]
            out_ref[x * NC + c] = total * factor_ref[x * NC + c]


def finish(parts, factor):
    return pl.pallas_call(
        finish_body,
        out_shape=jax.ShapeDtypeStruct((IRREPS, 32, SLOTS), jnp.float32),
        name="finish",
    )(parts, factor)


def factors(occ_energy, vir_energy, occ_irrep, vir_count):
    row_i = lax.axis_index("z") // 2
    row_a = (lax.axis_index("z") % 2 * NC + lax.axis_index("c")) * 32
    col_j = lax.axis_index("x") * NY + lax.axis_index("y")
    irreps = jnp.arange(IRREPS, dtype=jnp.int32)
    slots = jnp.arange(SLOTS, dtype=jnp.int32)

    def side(occupied):
        label = jnp.bitwise_xor(lax.dynamic_index_in_dim(occ_irrep, occupied, 0, False), irreps)
        onehot = label[:, None] == irreps[None, :]
        count = jnp.sum(jnp.where(onehot, vir_count[None, :], 0), axis=1)
        energy = jnp.sum(jnp.where(onehot[:, :, None], vir_energy[None], 0.0), axis=1)
        energy = lax.dynamic_index_in_dim(occ_energy, occupied, 0, False) - energy
        return energy, (slots[None, :] < count[:, None]).astype(jnp.float32)

    e_row, m_row = side(row_i)
    e_col, m_col = side(col_j)
    e_row = lax.dynamic_slice_in_dim(e_row, row_a, 32, 1)
    m_row = lax.dynamic_slice_in_dim(m_row, row_a, 32, 1)
    return m_row[:, :, None] * m_col[:, None, :] / (e_row[:, :, None] + e_col[:, None, :])


def on_device(t_cycle, w_cycle, occ_energy, vir_energy, occ_irrep, vir_count):
    own = lax.all_to_all(t_cycle, ("x", "c"), 0, 0, tiled=True)
    w_cycle, own = lax.optimization_barrier((w_cycle, own))
    up = shift_y(own, -1)
    down = shift_y(own, 1)
    across = shift_y(own, 4)
    w = lax.all_to_all(w_cycle, ("x", "c"), 0, 0, tiled=True)
    up_pair = shift_y(jnp.concatenate([up, across], axis=0), -1)
    down_pair = shift_y(jnp.concatenate([down, across], axis=0), 1)
    blocks = (own, up, down, across, up_pair, down_pair)
    partial = product(occ_irrep, vir_count, blocks, w)
    parts = lax.all_to_all(partial.reshape(NX * NZ * NC, 32, SLOTS), ("x", "z", "c"), 0, 0, tiled=True)
    factor = factors(occ_energy, vir_energy, occ_irrep, vir_count)
    return finish(parts.reshape(NX, NZ, NC, 32, SLOTS), factor)


def solution(mesh):
    grid = Mesh(mesh.devices.reshape(NX, NY, NZ, NC), AXES)
    return jax.shard_map(
        on_device,
        mesh=grid,
        in_specs=(P(None, ("x", "y"), ("z", "c")), P(None, ("z", "c"), ("x", "y")), P(), P(), P(), P()),
        out_specs=P(None, ("z", "c"), ("x", "y")),
        check_vma=False,
    )
```

```python
import functools

import jax
import jax.numpy as jnp
import numpy as np
from jax import lax
from jax.experimental import pallas as pl
from jax.experimental.pallas import tpu as pltpu
from jax.sharding import Mesh, PartitionSpec as P

IRREPS = 8
SLOTS = 128
NX, NY, NZ, NC = 4, 8, 8, 2
AXES = ("x", "y", "z", "c")
K_LOCAL = 512
OFFSETS = (0, 2, 6, 4)


IDS = np.arange(NX * NY * NZ * NC).reshape(NX, NY, NZ, NC)


def send(value, axis, first, second):
    targets = np.stack([np.roll(IDS[..., 0], -first, axis=axis), np.roll(IDS[..., 1], -second, axis=axis)], axis=-1)
    return lax.ppermute(value, AXES, list(zip(IDS.ravel().tolist(), targets.ravel().tolist())))


def split(value):
    high = value.astype(jnp.bfloat16)
    low = (value - high.astype(jnp.float32)).astype(jnp.bfloat16)
    return high, low


def product_body(first_half, occ_ref, count_ref, *refs):
    *t_refs, w_ref, same_ref, other_ref, t_high, t_low, w_high, w_low = refs
    y = lax.axis_index("y")
    z = lax.axis_index("z")
    c_own = lax.axis_index("c")
    g = lax.axis_index("x") * NC + c_own
    base = y if first_half else y + 1 + 6 * c_own

    for slot in range(4):
        ref, first = (t_refs[slot], 0) if first_half else (t_refs[0], slot * 8)
        for i in range(NX):
            for c in range(NC):
                high, low = split(ref[first + i * NC + c])
                rows = pl.ds((slot * NX + i) * 16, 16)
                cols = pl.ds(c * K_LOCAL, K_LOCAL)
                t_high[rows, cols] = high
                t_low[rows, cols] = low

    slots = lax.broadcasted_iota(jnp.int32, (SLOTS, SLOTS), 0)
    for c in range(NC):
        for k in range(4):
            live = slots < count_ref[jnp.bitwise_xor(occ_ref[z * 8 + c * 4 + k], g)]
            for col in range(NX):
                part = jnp.where(live, w_ref[col * NC + c, pl.ds(k * SLOTS, SLOTS), :], 0.0)
                high, low = split(part)
                rows = pl.ds(c * K_LOCAL + k * SLOTS, SLOTS)
                cols = pl.ds(col * SLOTS, SLOTS)
                w_high[rows, cols] = high
                w_low[rows, cols] = low

    def dot(a, b):
        return jnp.dot(a[...], b[...], preferred_element_type=jnp.float32)

    total = dot(t_high, w_low) + dot(t_low, w_high) + dot(t_high, w_high)
    for slot, offset in enumerate(OFFSETS):
        quarter = lax.rem(base + offset, NY) // 2
        for i in range(NX):
            for col in range(NX):
                rows = slice((slot * NX + i) * 16, (slot * NX + i + 1) * 16)
                value = total[rows, col * SLOTS : (col + 1) * SLOTS]
                if first_half:
                    same_ref[col, i * 4 + quarter] = value
                else:
                    spot = i * NC + lax.rem(quarter, 2)
                    mine = lax.rem(quarter // 2 + z, 2) == 0

                    @pl.when(mine)
                    def _():
                        same_ref[col, spot] = value

                    @pl.when(jnp.logical_not(mine))
                    def _():
                        other_ref[col, spot] = value


def product(first_half, occ_irrep, vir_count, blocks, w):
    shape = jax.ShapeDtypeStruct((NX, 16 if first_half else 8, 16, SLOTS), jnp.float32)
    body = functools.partial(product_body, first_half)
    if first_half:
        body = lambda *refs: product_body(True, *refs[:8], None, *refs[8:])
    return pl.pallas_call(
        body,
        in_specs=[pl.BlockSpec(memory_space=pltpu.SMEM)] * 2
        + [pl.BlockSpec(memory_space=pltpu.VMEM)] * (len(blocks) + 1),
        out_shape=shape if first_half else (shape, shape),
        scratch_shapes=[
            pltpu.VMEM((256, 2 * K_LOCAL), jnp.bfloat16),
            pltpu.VMEM((256, 2 * K_LOCAL), jnp.bfloat16),
            pltpu.VMEM((2 * K_LOCAL, NX * SLOTS), jnp.bfloat16),
            pltpu.VMEM((2 * K_LOCAL, NX * SLOTS), jnp.bfloat16),
        ],
        name="first_product" if first_half else "second_product",
    )(occ_irrep, vir_count, *blocks, w)


def finish_body(first_ref, second_ref, factor_ref, out_ref):
    parity = lax.rem(lax.axis_index("y"), 2)
    for ref, part in ((first_ref, parity), (second_ref, 1 - parity)):
        rows = pl.ds(pl.multiple_of(part * 16, 16), 16)
        for x in range(NX):
            for c in range(NC):
                total = ref[x, 0, c]
                for z in range(1, ref.shape[1]):
                    total = total + ref[x, z, c]
                out_ref[x * NC + c, rows, :] = total * factor_ref[x * NC + c, rows, :]


def finish(first, second, factor):
    return pl.pallas_call(
        finish_body,
        out_shape=jax.ShapeDtypeStruct((IRREPS, 32, SLOTS), jnp.float32),
        name="finish",
    )(first, second, factor)


def factors(occ_energy, vir_energy, occ_irrep, vir_count):
    row_i = lax.axis_index("z") // 2
    row_a = (lax.axis_index("z") % 2 * NC + lax.axis_index("c")) * 32
    col_j = lax.axis_index("x") * NY + lax.axis_index("y")
    irreps = jnp.arange(IRREPS, dtype=jnp.int32)
    slots = jnp.arange(SLOTS, dtype=jnp.int32)

    def side(occupied):
        label = jnp.bitwise_xor(lax.dynamic_index_in_dim(occ_irrep, occupied, 0, False), irreps)
        onehot = label[:, None] == irreps[None, :]
        count = jnp.sum(jnp.where(onehot, vir_count[None, :], 0), axis=1)
        energy = jnp.sum(jnp.where(onehot[:, :, None], vir_energy[None], 0.0), axis=1)
        energy = lax.dynamic_index_in_dim(occ_energy, occupied, 0, False) - energy
        return energy, (slots[None, :] < count[:, None]).astype(jnp.float32)

    e_row, m_row = side(row_i)
    e_col, m_col = side(col_j)
    e_row = lax.dynamic_slice_in_dim(e_row, row_a, 32, 1)
    m_row = lax.dynamic_slice_in_dim(m_row, row_a, 32, 1)
    return m_row[:, :, None] * m_col[:, None, :] / (e_row[:, :, None] + e_col[:, None, :])


def on_device(t_cycle, w_cycle, occ_energy, vir_energy, occ_irrep, vir_count):
    own = lax.all_to_all(t_cycle, ("x", "c"), 0, 0, tiled=True)
    w_cycle, own = lax.optimization_barrier((w_cycle, own))
    w = lax.all_to_all(w_cycle, ("x", "c"), 0, 0, tiled=True)
    blocks = (own, send(own, 1, -2, -2), send(own, 1, 2, 2), send(own, 1, 4, 4))
    others = send(jnp.concatenate(blocks, axis=0), 1, -1, 1)
    first = product(True, occ_irrep, vir_count, blocks, w)
    first = lax.all_to_all(first.reshape(NX * NZ * NC, 16, SLOTS), ("x", "z", "c"), 0, 0, tiled=True)
    same, other = product(False, occ_irrep, vir_count, (others,), w)
    arrived = send(other, 2, 1, -1)
    second = same + arrived
    peers = np.moveaxis(IDS.reshape(NX, NY, NZ // 2, 2, NC), (1, 3), (0, 1)).reshape(NY * 2, -1)
    second = lax.all_to_all(
        second.reshape(NX * NZ // 2 * NC, 16, SLOTS), AXES, 0, 0, tiled=True, axis_index_groups=peers.tolist()
    )
    factor = factors(occ_energy, vir_energy, occ_irrep, vir_count)
    return finish(first.reshape(NX, NZ, NC, 16, SLOTS), second.reshape(NX, NZ // 2, NC, 16, SLOTS), factor)


def solution(mesh):
    grid = Mesh(mesh.devices.reshape(NX, NY, NZ, NC), AXES)
    return jax.shard_map(
        on_device,
        mesh=grid,
        in_specs=(P(None, ("x", "y"), ("z", "c")), P(None, ("z", "c"), ("x", "y")), P(), P(), P(), P()),
        out_specs=P(None, ("z", "c"), ("x", "y")),
        check_vma=False,
    )
```

```python
import jax
import jax.numpy as jnp
import numpy as np
from jax import lax
from jax.experimental import pallas as pl
from jax.experimental.pallas import tpu as pltpu
from jax.sharding import Mesh, PartitionSpec as P

IRREPS = 8
SLOTS = 128
NX, NY, NZ, NC = 4, 8, 8, 2
AXES = ("x", "y", "z", "c")
K_LOCAL = 512
OFFSETS = (0, 1, 7, 2, 6, 3, 5, 4)


IDS = np.arange(NX * NY * NZ * NC).reshape(NX, NY, NZ, NC)


def send(value, axis, first, second):
    targets = np.stack([np.roll(IDS[..., 0], -first, axis=axis), np.roll(IDS[..., 1], -second, axis=axis)], axis=-1)
    return lax.ppermute(value, AXES, list(zip(IDS.ravel().tolist(), targets.ravel().tolist())))


def split(value):
    high = value.astype(jnp.bfloat16)
    low = (value - high.astype(jnp.float32)).astype(jnp.bfloat16)
    return high, low


def product_body(occ_ref, count_ref, *refs):
    *t_refs, w_ref, out_ref, t_high, t_low, w_high, w_low = refs
    y = lax.axis_index("y")
    z = lax.axis_index("z")
    g = lax.axis_index("x") * NC + lax.axis_index("c")
    for slot, ref in enumerate(t_refs):
        for i in range(NX):
            for c in range(NC):
                high, low = split(ref[i * NC + c])
                rows = pl.ds((slot * NX + i) * 16, 16)
                cols = pl.ds(c * K_LOCAL, K_LOCAL)
                t_high[rows, cols] = high
                t_low[rows, cols] = low

    slots = lax.broadcasted_iota(jnp.int32, (SLOTS, SLOTS), 0)
    for c in range(NC):
        for k in range(4):
            live = slots < count_ref[jnp.bitwise_xor(occ_ref[z * 8 + c * 4 + k], g)]
            for col in range(NX):
                part = jnp.where(live, w_ref[col * NC + c, pl.ds(k * SLOTS, SLOTS), :], 0.0)
                high, low = split(part)
                rows = pl.ds(c * K_LOCAL + k * SLOTS, SLOTS)
                cols = pl.ds(col * SLOTS, SLOTS)
                w_high[rows, cols] = high
                w_low[rows, cols] = low

    def dot(a, b):
        return jnp.dot(a[...], b[...], preferred_element_type=jnp.float32)

    total = dot(t_high, w_low) + dot(t_low, w_high) + dot(t_high, w_high)
    for slot, offset in enumerate(OFFSETS):
        first = pl.multiple_of(lax.rem(y + offset, NY) * 16, 16)
        for i in range(NX):
            rows = slice((slot * NX + i) * 16, (slot * NX + i + 1) * 16)
            for col in range(NX):
                out_ref[col, i, pl.ds(first, 16), :] = total[rows, col * SLOTS : (col + 1) * SLOTS]


def product(occ_irrep, vir_count, blocks, w):
    return pl.pallas_call(
        product_body,
        in_specs=[pl.BlockSpec(memory_space=pltpu.SMEM)] * 2
        + [pl.BlockSpec(memory_space=pltpu.VMEM)] * (len(blocks) + 1),
        out_shape=jax.ShapeDtypeStruct((NX, NX, SLOTS, SLOTS), jnp.float32),
        scratch_shapes=[
            pltpu.VMEM((512, 2 * K_LOCAL), jnp.bfloat16),
            pltpu.VMEM((512, 2 * K_LOCAL), jnp.bfloat16),
            pltpu.VMEM((2 * K_LOCAL, NX * SLOTS), jnp.bfloat16),
            pltpu.VMEM((2 * K_LOCAL, NX * SLOTS), jnp.bfloat16),
        ],
        name="product",
    )(occ_irrep, vir_count, *blocks, pltpu.with_memory_space_constraint(w, pltpu.VMEM))


def finish_body(parts_ref, factor_ref, out_ref):
    for x in range(NX):
        for c in range(NC):
            total = parts_ref[x, 0, c]
            for z in range(1, NZ):
                total = total + parts_ref[x, z, c]
            out_ref[x * NC + c] = total * factor_ref[x * NC + c]


def finish(parts, factor):
    return pl.pallas_call(
        finish_body,
        in_specs=[pl.BlockSpec(memory_space=pltpu.VMEM)] * 2,
        out_shape=jax.ShapeDtypeStruct((IRREPS, 32, SLOTS), jnp.float32),
        name="finish",
    )(pltpu.with_memory_space_constraint(parts, pltpu.VMEM), factor)


def factors(occ_energy, vir_energy, occ_irrep, vir_count):
    row_i = lax.axis_index("z") // 2
    row_a = (lax.axis_index("z") % 2 * NC + lax.axis_index("c")) * 32
    col_j = lax.axis_index("x") * NY + lax.axis_index("y")
    irreps = jnp.arange(IRREPS, dtype=jnp.int32)
    slots = jnp.arange(SLOTS, dtype=jnp.int32)

    def side(occupied):
        label = jnp.bitwise_xor(lax.dynamic_index_in_dim(occ_irrep, occupied, 0, False), irreps)
        onehot = label[:, None] == irreps[None, :]
        count = jnp.sum(jnp.where(onehot, vir_count[None, :], 0), axis=1)
        energy = jnp.sum(jnp.where(onehot[:, :, None], vir_energy[None], 0.0), axis=1)
        energy = lax.dynamic_index_in_dim(occ_energy, occupied, 0, False) - energy
        return energy, (slots[None, :] < count[:, None]).astype(jnp.float32)

    e_row, m_row = side(row_i)
    e_col, m_col = side(col_j)
    e_row = lax.dynamic_slice_in_dim(e_row, row_a, 32, 1)
    m_row = lax.dynamic_slice_in_dim(m_row, row_a, 32, 1)
    return m_row[:, :, None] * m_col[:, None, :] / (e_row[:, :, None] + e_col[:, None, :])


def on_device(t_cycle, w_cycle, occ_energy, vir_energy, occ_irrep, vir_count):
    own = lax.all_to_all(t_cycle, ("x", "c"), 0, 0, tiled=True)
    w_cycle, own = lax.optimization_barrier((w_cycle, own))
    w = lax.all_to_all(w_cycle, ("x", "c"), 0, 0, tiled=True)
    across = send(own, 1, 4, 4)
    blocks, up, down = [own], own, own
    for _ in range(3):
        up = send(up, 1, -1, -1)
        down = send(down, 1, 1, 1)
        blocks += [up, down]
    blocks.append(across)
    partial = product(occ_irrep, vir_count, blocks, w)
    parts = lax.all_to_all(partial.reshape(NX * NZ * NC, 32, SLOTS), ("x", "z", "c"), 0, 0, tiled=True)
    factor = factors(occ_energy, vir_energy, occ_irrep, vir_count)
    return finish(parts.reshape(NX, NZ, NC, 32, SLOTS), factor)


def solution(mesh):
    grid = Mesh(mesh.devices.reshape(NX, NY, NZ, NC), AXES)
    return jax.shard_map(
        on_device,
        mesh=grid,
        in_specs=(P(None, ("x", "y"), ("z", "c")), P(None, ("z", "c"), ("x", "y")), P(), P(), P(), P()),
        out_specs=P(None, ("z", "c"), ("x", "y")),
        check_vma=False,
    )
```

```python
import jax
import jax.numpy as jnp
import numpy as np
from jax import lax
from jax.experimental import pallas as pl
from jax.experimental.pallas import tpu as pltpu
from jax.sharding import Mesh, PartitionSpec as P

IRREPS = 8
SLOTS = 128
NX, NY, NZ, NC = 4, 8, 8, 2
AXES = ("x", "y", "z", "c")
K_LOCAL = 512
OFFSETS = (0, 1, 7, 4, 2, 5, 6, 3)


IDS = np.arange(NX * NY * NZ * NC).reshape(NX, NY, NZ, NC)


def send(value, axis, first, second):
    targets = np.stack([np.roll(IDS[..., 0], -first, axis=axis), np.roll(IDS[..., 1], -second, axis=axis)], axis=-1)
    return lax.ppermute(value, AXES, list(zip(IDS.ravel().tolist(), targets.ravel().tolist())))


def split(value):
    high = value.astype(jnp.bfloat16)
    low = (value - high.astype(jnp.float32)).astype(jnp.bfloat16)
    return high, low


def split_rows(t_in, t_high, t_low):
    for n in range(4):
        for i in range(NX):
            for c in range(NC):
                high, low = split(t_in[n * 8 + i * NC + c])
                rows = pl.ds((n * NX + i) * 16, 16)
                cols = pl.ds(c * K_LOCAL, K_LOCAL)
                t_high[rows, cols] = high
                t_low[rows, cols] = low


def multiply(t_high, t_low, w_high, w_low):
    def dot(a, b):
        return jnp.dot(a[...], b[...], preferred_element_type=jnp.float32)

    return dot(t_high, w_low) + dot(t_low, w_high) + dot(t_high, w_high)


def first_body(occ_ref, count_ref, *refs):
    *t_refs, w_ref, out_ref, w_high, w_low, t_in, t_high, t_low, sems = refs
    y = lax.axis_index("y")
    z = lax.axis_index("z")
    g = lax.axis_index("x") * NC + lax.axis_index("c")
    copies = [pltpu.make_async_copy(ref, t_in.at[pl.ds(n * 8, 8)], sems.at[n]) for n, ref in enumerate(t_refs)]
    for copy in copies:
        copy.start()
    slots = lax.broadcasted_iota(jnp.int32, (SLOTS, SLOTS), 0)
    for c in range(NC):
        for k in range(4):
            live = slots < count_ref[jnp.bitwise_xor(occ_ref[z * 8 + c * 4 + k], g)]
            for col in range(NX):
                part = jnp.where(live, w_ref[col * NC + c, pl.ds(k * SLOTS, SLOTS), :], 0.0)
                high, low = split(part)
                rows = pl.ds(c * K_LOCAL + k * SLOTS, SLOTS)
                cols = pl.ds(col * SLOTS, SLOTS)
                w_high[rows, cols] = high
                w_low[rows, cols] = low
    for copy in copies:
        copy.wait()
    split_rows(t_in, t_high, t_low)
    total = multiply(t_high, t_low, w_high, w_low)
    for n in range(4):
        first = pl.multiple_of(lax.rem(y + OFFSETS[n], NY) * 16, 16)
        for i in range(NX):
            for col in range(NX):
                rows = slice((n * NX + i) * 16, (n * NX + i + 1) * 16)
                out_ref[col, i, pl.ds(first, 16), :] = total[rows, col * SLOTS : (col + 1) * SLOTS]


def second_body(partial_ref, t0, t1, w_high, w_low, out_ref, t_in, t_high, t_low, rows_out, sems):
    del partial_ref
    y = lax.axis_index("y")
    t_copies = [pltpu.make_async_copy(ref, t_in.at[pl.ds(n * 16, 16)], sems.at[n]) for n, ref in enumerate((t0, t1))]
    for copy in t_copies:
        copy.start()
    for copy in t_copies:
        copy.wait()
    split_rows(t_in, t_high, t_low)
    total = multiply(t_high, t_low, w_high, w_low)
    out_copies = []
    for n in range(4):
        first = pl.multiple_of(lax.rem(y + OFFSETS[4 + n], NY) * 16, 16)
        for i in range(NX):
            for col in range(NX):
                rows = slice((n * NX + i) * 16, (n * NX + i + 1) * 16)
                rows_out[n, col, i] = total[rows, col * SLOTS : (col + 1) * SLOTS]
        out_copies.append(pltpu.make_async_copy(rows_out.at[n], out_ref.at[:, :, pl.ds(first, 16), :], sems.at[2 + n]))
        out_copies[-1].start()
    for copy in out_copies:
        copy.wait()


def product(occ_irrep, vir_count, blocks, w):
    anywhere = pl.BlockSpec(memory_space=pl.ANY)
    shape = jax.ShapeDtypeStruct((NX, NX, SLOTS, SLOTS), jnp.float32)
    w_part = jax.ShapeDtypeStruct((2 * K_LOCAL, NX * SLOTS), jnp.bfloat16)
    t_in = pltpu.VMEM((32, 16, K_LOCAL), jnp.float32)
    t_part = pltpu.VMEM((256, 2 * K_LOCAL), jnp.bfloat16)
    partial, w_high, w_low = pl.pallas_call(
        first_body,
        in_specs=[pl.BlockSpec(memory_space=pltpu.SMEM)] * 2
        + [anywhere] * 4
        + [pl.BlockSpec(memory_space=pltpu.VMEM)],
        out_shape=(shape, w_part, w_part),
        scratch_shapes=[t_in, t_part, t_part, pltpu.SemaphoreType.DMA((4,))],
        name="first_product",
    compiler_params=pltpu.CompilerParams(vmem_limit_bytes=20 * 2**20),
    )(occ_irrep, vir_count, *blocks[:4], pltpu.with_memory_space_constraint(w, pltpu.VMEM))
    return pl.pallas_call(
        second_body,
        in_specs=[anywhere] * 3 + [pl.BlockSpec(memory_space=pltpu.VMEM)] * 2,
        out_specs=anywhere,
        out_shape=shape,
        scratch_shapes=[
            t_in,
            t_part,
            t_part,
            pltpu.VMEM((4, NX, NX, 16, SLOTS), jnp.float32),
            pltpu.SemaphoreType.DMA((6,)),
        ],
        input_output_aliases={0: 0},
        name="second_product",
    compiler_params=pltpu.CompilerParams(vmem_limit_bytes=20 * 2**20),
    )(partial, *blocks[4:], *[pltpu.with_memory_space_constraint(v, pltpu.VMEM) for v in (w_high, w_low)])


def finish_body(parts_ref, factor_ref, out_ref):
    for x in range(NX):
        for c in range(NC):
            total = parts_ref[x, 0, c]
            for z in range(1, NZ):
                total = total + parts_ref[x, z, c]
            out_ref[x * NC + c] = total * factor_ref[x * NC + c]


def finish(parts, factor):
    return pl.pallas_call(
        finish_body,
        in_specs=[pl.BlockSpec(memory_space=pltpu.VMEM)] * 2,
        out_shape=jax.ShapeDtypeStruct((IRREPS, 32, SLOTS), jnp.float32),
        name="finish",
        compiler_params=pltpu.CompilerParams(vmem_limit_bytes=16 * 2**20),
    )(pltpu.with_memory_space_constraint(parts, pltpu.VMEM), factor)


def factors(occ_energy, vir_energy, occ_irrep, vir_count):
    row_i = lax.axis_index("z") // 2
    row_a = (lax.axis_index("z") % 2 * NC + lax.axis_index("c")) * 32
    col_j = lax.axis_index("x") * NY + lax.axis_index("y")
    irreps = jnp.arange(IRREPS, dtype=jnp.int32)
    slots = jnp.arange(SLOTS, dtype=jnp.int32)

    def side(occupied):
        label = jnp.bitwise_xor(lax.dynamic_index_in_dim(occ_irrep, occupied, 0, False), irreps)
        onehot = label[:, None] == irreps[None, :]
        count = jnp.sum(jnp.where(onehot, vir_count[None, :], 0), axis=1)
        energy = jnp.sum(jnp.where(onehot[:, :, None], vir_energy[None], 0.0), axis=1)
        energy = lax.dynamic_index_in_dim(occ_energy, occupied, 0, False) - energy
        return energy, (slots[None, :] < count[:, None]).astype(jnp.float32)

    e_row, m_row = side(row_i)
    e_col, m_col = side(col_j)
    e_row = lax.dynamic_slice_in_dim(e_row, row_a, 32, 1)
    m_row = lax.dynamic_slice_in_dim(m_row, row_a, 32, 1)
    return m_row[:, :, None] * m_col[:, None, :] / (e_row[:, :, None] + e_col[:, None, :])


def on_device(t_cycle, w_cycle, occ_energy, vir_energy, occ_irrep, vir_count):
    own = lax.all_to_all(t_cycle, ("x", "c"), 0, 0, tiled=True)
    w_cycle, own = lax.optimization_barrier((w_cycle, own))
    w = lax.all_to_all(w_cycle, ("x", "c"), 0, 0, tiled=True)
    across = send(own, 1, 4, 4)
    blocks, up, down = [own], own, own
    up = send(up, 1, -1, -1)
    down = send(down, 1, 1, 1)
    blocks += [up, down, across]
    blocks.append(send(jnp.concatenate([up, across]), 1, -1, -1))
    blocks.append(send(jnp.concatenate([down, across]), 1, 1, 1))
    partial = product(occ_irrep, vir_count, blocks, w)
    parts = lax.all_to_all(partial.reshape(NX * NZ * NC, 32, SLOTS), ("x", "z", "c"), 0, 0, tiled=True)
    factor = factors(occ_energy, vir_energy, occ_irrep, vir_count)
    return finish(parts.reshape(NX, NZ, NC, 32, SLOTS), factor)


def solution(mesh):
    grid = Mesh(mesh.devices.reshape(NX, NY, NZ, NC), AXES)
    return jax.shard_map(
        on_device,
        mesh=grid,
        in_specs=(P(None, ("x", "y"), ("z", "c")), P(None, ("z", "c"), ("x", "y")), P(), P(), P(), P()),
        out_specs=P(None, ("z", "c"), ("x", "y")),
        check_vma=False,
    )
```

```python
import jax
import jax.numpy as jnp
import numpy as np
from jax import lax
from jax.experimental import pallas as pl
from jax.experimental.pallas import tpu as pltpu
from jax.sharding import Mesh, PartitionSpec as P

IRREPS = 8
SLOTS = 128
NX, NY, NZ, NC = 4, 8, 8, 2
AXES = ("x", "y", "z", "c")
K_LOCAL = 512
OFFSETS = (0, 1, 7, 4, 2, 6, 5, 3)


IDS = np.arange(NX * NY * NZ * NC).reshape(NX, NY, NZ, NC)


def send(value, axis, first, second):
    targets = np.stack([np.roll(IDS[..., 0], -first, axis=axis), np.roll(IDS[..., 1], -second, axis=axis)], axis=-1)
    return lax.ppermute(value, AXES, list(zip(IDS.ravel().tolist(), targets.ravel().tolist())))


def split(value):
    high = value.astype(jnp.bfloat16)
    low = (value - high.astype(jnp.float32)).astype(jnp.bfloat16)
    return high, low


def product_body(occ_ref, count_ref, *refs):
    *t_refs, w_ref, out_ref, t_in, t_high, t_low, w_high, w_low, total, sems = refs
    y = lax.axis_index("y")
    z = lax.axis_index("z")
    g = lax.axis_index("x") * NC + lax.axis_index("c")
    arrivals = [pltpu.make_async_copy(ref, t_in.at[slot], sems.at[slot]) for slot, ref in enumerate(t_refs)]
    for copy in arrivals:
        copy.start()
    slots = lax.broadcasted_iota(jnp.int32, (SLOTS, SLOTS), 0)

    def dot(a, b):
        return jnp.dot(a[...], b[...], preferred_element_type=jnp.float32)

    for half in range(2):
        for c in range(NC):
            for k in range(4):
                live = slots < count_ref[jnp.bitwise_xor(occ_ref[z * 8 + c * 4 + k], g)]
                for col in range(2):
                    part = w_ref[(half * 2 + col) * NC + c, pl.ds(k * SLOTS, SLOTS), :]
                    high, low = split(jnp.where(live, part, 0.0))
                    rows = pl.ds(c * K_LOCAL + k * SLOTS, SLOTS)
                    cols = pl.ds(col * SLOTS, SLOTS)
                    w_high[half, rows, cols] = high
                    w_low[half, rows, cols] = low
    for slot, copy in enumerate(arrivals):
        copy.wait()
        first = lax.rem(y + OFFSETS[slot], NY) * 16
        for i in range(NX):
            for c in range(NC):
                high, low = split(t_in[slot, i * NC + c])
                rows = pl.ds(pl.multiple_of(i * SLOTS + first, 16), 16)
                cols = pl.ds(c * K_LOCAL, K_LOCAL)
                t_high[rows, cols] = high
                t_low[rows, cols] = low
    departures = []
    for half in range(2):
        high, low = w_high.at[half], w_low.at[half]
        value = dot(t_high, low) + dot(t_low, high) + dot(t_high, high)
        for col in range(2):
            total[half * 2 + col] = value[:, col * SLOTS : (col + 1) * SLOTS]
        spot = pl.ds(half * 2, 2)
        departures.append(pltpu.make_async_copy(total.at[spot], out_ref.at[spot], sems.at[8 + half]))
        departures[-1].start()
    for copy in departures:
        copy.wait()


def product(occ_irrep, vir_count, blocks, w):
    anywhere = pl.BlockSpec(memory_space=pl.ANY)
    t_part = pltpu.VMEM((512, 2 * K_LOCAL), jnp.bfloat16)
    w_part = pltpu.VMEM((2, 2 * K_LOCAL, 2 * SLOTS), jnp.bfloat16)
    return pl.pallas_call(
        product_body,
        in_specs=[pl.BlockSpec(memory_space=pltpu.SMEM)] * 2
        + [anywhere] * 8
        + [pl.BlockSpec(memory_space=pltpu.VMEM)],
        out_specs=anywhere,
        out_shape=jax.ShapeDtypeStruct((NX, NX * SLOTS, SLOTS), jnp.float32),
        scratch_shapes=[
            pltpu.VMEM((8, 8, 16, K_LOCAL), jnp.float32),
            t_part,
            t_part,
            w_part,
            w_part,
            pltpu.VMEM((NX, NX * SLOTS, SLOTS), jnp.float32),
            pltpu.SemaphoreType.DMA((10,)),
        ],
        compiler_params=pltpu.CompilerParams(vmem_limit_bytes=24 * 2**20),
        name="product",
    )(occ_irrep, vir_count, *blocks[:5], *[pltpu.with_memory_space_constraint(b, pltpu.HBM) for b in blocks[5:]], pltpu.with_memory_space_constraint(w, pltpu.VMEM))


def finish_body(parts_ref, factor_ref, out_ref):
    for x in range(NX):
        for c in range(NC):
            total = parts_ref[x, 0, c]
            for z in range(1, NZ):
                total = total + parts_ref[x, z, c]
            out_ref[x * NC + c] = total * factor_ref[x * NC + c]


def finish(parts, factor):
    return pl.pallas_call(
        finish_body,
        in_specs=[pl.BlockSpec(memory_space=pltpu.VMEM)] * 2,
        out_shape=jax.ShapeDtypeStruct((IRREPS, 32, SLOTS), jnp.float32),
        name="finish",
        compiler_params=pltpu.CompilerParams(vmem_limit_bytes=16 * 2**20),
    )(pltpu.with_memory_space_constraint(parts, pltpu.VMEM), factor)


def factors(occ_energy, vir_energy, occ_irrep, vir_count):
    row_i = lax.axis_index("z") // 2
    row_a = (lax.axis_index("z") % 2 * NC + lax.axis_index("c")) * 32
    col_j = lax.axis_index("x") * NY + lax.axis_index("y")
    irreps = jnp.arange(IRREPS, dtype=jnp.int32)
    slots = jnp.arange(SLOTS, dtype=jnp.int32)

    def side(occupied):
        label = jnp.bitwise_xor(lax.dynamic_index_in_dim(occ_irrep, occupied, 0, False), irreps)
        onehot = label[:, None] == irreps[None, :]
        count = jnp.sum(jnp.where(onehot, vir_count[None, :], 0), axis=1)
        energy = jnp.sum(jnp.where(onehot[:, :, None], vir_energy[None], 0.0), axis=1)
        energy = lax.dynamic_index_in_dim(occ_energy, occupied, 0, False) - energy
        return energy, (slots[None, :] < count[:, None]).astype(jnp.float32)

    e_row, m_row = side(row_i)
    e_col, m_col = side(col_j)
    e_row = lax.dynamic_slice_in_dim(e_row, row_a, 32, 1)
    m_row = lax.dynamic_slice_in_dim(m_row, row_a, 32, 1)
    return m_row[:, :, None] * m_col[:, None, :] / (e_row[:, :, None] + e_col[:, None, :])


def on_device(t_cycle, w_cycle, occ_energy, vir_energy, occ_irrep, vir_count):
    own = lax.all_to_all(t_cycle, ("x", "c"), 0, 0, tiled=True)
    w_cycle, own = lax.optimization_barrier((w_cycle, own))
    w = lax.all_to_all(w_cycle, ("x", "c"), 0, 0, tiled=True)
    across = send(own, 1, 4, 4)
    blocks, up, down = [own], own, own
    up = send(up, 1, -1, -1)
    down = send(down, 1, 1, 1)
    blocks += [up, down, across]
    blocks.append(send(up, 1, -1, -1))
    blocks.append(send(down, 1, 1, 1))
    blocks.append(send(across, 1, -1, -1))
    blocks.append(send(across, 1, 1, 1))
    partial = product(occ_irrep, vir_count, blocks, w)
    parts = lax.all_to_all(partial.reshape(NX * NZ * NC, 32, SLOTS), ("x", "z", "c"), 0, 0, tiled=True)
    factor = factors(occ_energy, vir_energy, occ_irrep, vir_count)
    return finish(parts.reshape(NX, NZ, NC, 32, SLOTS), factor)


def solution(mesh):
    grid = Mesh(mesh.devices.reshape(NX, NY, NZ, NC), AXES)
    return jax.shard_map(
        on_device,
        mesh=grid,
        in_specs=(P(None, ("x", "y"), ("z", "c")), P(None, ("z", "c"), ("x", "y")), P(), P(), P(), P()),
        out_specs=P(None, ("z", "c"), ("x", "y")),
        check_vma=False,
    )
```
